512 devices in a mesh: dp: 64 (over z, x_hi, core), coef: 8 (over y, x_lo).
Axes of the slice: x: 4 (x_hi: 2, x_lo: 2; x = x_hi * 2 + x_lo), y: 4, z: 16, core: 2. Of those that a mesh axis runs over, the one named last changes fastest.
Arguments:
- location: int32 [32768], P('dp'), may hold values from 0 to 1023
- component: int32 [32768], P('dp'), may hold values from 0 to 2
- epoch_bin: int32 [32768], P('dp'), may hold values from 0 to 127
- residual: bfloat16 [32768], P('dp'), may hold values from -6 to 6
- row_scale: bfloat16 [32768], P('dp'), may hold values from 0.5 to 2
- spatial_table: bfloat16 [3072, 3072], P(None, 'coef'), may hold values from -1 to 3
- spline_table: bfloat16 [128, 3072], P(None, 'coef'), may hold values from 0 to 1
Outputs:
- gram_band: float32 [8, 384, 1920], P('coef', 'dp')
- gradient: float32 [8, 384], P('coef', 'dp')
The draws below stay inside these ranges and needn't reach their ends.
All inputs are finite; a program needn't handle non-finite values.
Results may differ from the reference program's by a relative error of at most 0.0042.
The reference program's roundings to bfloat16 on the way (of `design` and `whitened`) count: a program that leaves them out, or rounds other values in their place, can miss the bound.
Values may be sent and summed in bfloat16 or wider, within the bound.
A program may use at most 64 MiB of HBM per device.

```python
import math
import jax
import jax.numpy as jnp
from jax import lax

COEFFS = 3072
NLOC = 1024
NSP = 3072
NEP = 128
ROWS_DEV = 512
ROWS = 32768
PAN = 384
N_DP = 64
N_COEF = 8


def plant(drawn, stream_key, low, top_value):
    extent = drawn.shape
    index_at = [jax.random.randint(jax.random.fold_in(stream_key, axis), (), 0, extent[axis]) for axis in range(len(extent))]
    drawn = drawn.at[tuple(index_at)].set(low)
    longest = extent.index(max(extent))
    index_at[longest] = (index_at[longest] + 1) % extent[longest]
    return drawn.at[tuple(index_at)].set(top_value)


def block_scale(own_key, extent, split, smallest, top_value):
    def one(position, blocks):
        steps = jax.random.uniform(jax.random.fold_in(jax.random.fold_in(own_key, 6), position), (blocks,), jnp.float32, smallest / len(split), top_value / len(split))
        return jnp.repeat(jnp.exp(steps), extent[position] // blocks).reshape((-1,) + (1,) * (len(extent) - position - 1))

    level = one(*split[0])
    for cut in split[1:]:
        level = level * one(*cut)
    return level


def noise(rng, extent, spread, bound, cuts=(), kind=jnp.bfloat16):
    array = spread * jax.random.normal(rng, extent, jnp.float32)
    if cuts:
        array = array * block_scale(rng, extent, cuts, -0.22, 0.18)
    return jnp.clip(array, -bound, bound).astype(kind)


def setup_inputs(seed: int = 0) -> dict:
    key_of = jax.random.split(jax.random.key(seed), 8)
    location = plant(jax.random.randint(key_of[0], (ROWS,), 0, NLOC), jax.random.fold_in(key_of[0], 1), 0, NLOC - 1).astype(jnp.int32)
    component = plant(jax.random.randint(key_of[1], (ROWS,), 0, 3), jax.random.fold_in(key_of[1], 1), 0, 2).astype(jnp.int32)
    epoch_bin = plant(jax.random.randint(key_of[2], (ROWS,), 0, NEP), jax.random.fold_in(key_of[2], 1), 0, NEP - 1).astype(jnp.int32)
    residual = noise(key_of[3], (ROWS,), 1.0, 6.0, ((0, 64),))
    row_scale = jnp.clip(jnp.exp(math.log(2.0) - 1.3862944 * jax.random.uniform(key_of[4], (ROWS,), jnp.float32) ** block_scale(key_of[4], (ROWS,), ((0, 64),), -0.2, 0.2)), 0.5, 2.0).astype(jnp.bfloat16)
    spatial_table = jnp.clip(-1.0 + 4.0 * jax.random.uniform(key_of[5], (NSP, COEFFS), jnp.float32) ** block_scale(key_of[5], (NSP, COEFFS), ((1, 8),), -0.2, 0.2), -1.0, 3.0).astype(jnp.bfloat16)
    spline_table = jnp.clip(1.0 * jax.random.uniform(key_of[6], (NEP, COEFFS), jnp.float32) ** block_scale(key_of[6], (NEP, COEFFS), ((1, 8),), -0.2, 0.2), 0.0, 1.0).astype(jnp.bfloat16)
    return dict(location=location, component=component, epoch_bin=epoch_bin, residual=residual, row_scale=row_scale, spatial_table=spatial_table, spline_table=spline_table)


def reference(location, component, epoch_bin, residual, row_scale, spatial_table, spline_table):
    row_weight = row_scale.astype(jnp.float32) * (1.0 / math.sqrt(ROWS))
    whitened = (row_scale.astype(jnp.float32) * residual.astype(jnp.float32)).astype(jnp.bfloat16)
    spatial_index = (3 * location + component).astype(jnp.int32)

    def accumulate(totals, row_block):
        normal, gradient = totals
        spatial_rows, spline_rows, weight_rows, white_rows = row_block
        spatial_value = jnp.take(spatial_table, spatial_rows, axis=0).astype(jnp.float32)
        spline_value = jnp.take(spline_table, spline_rows, axis=0).astype(jnp.float32)
        design = (spatial_value * spline_value * weight_rows[:, None]).astype(jnp.bfloat16)
        normal = normal + jnp.dot(design.T, design, preferred_element_type=jnp.float32)
        gradient = gradient + jnp.dot(design.T, white_rows, preferred_element_type=jnp.float32)
        return ((normal, gradient), None)
    blocks = (spatial_index.reshape(N_DP, ROWS_DEV), epoch_bin.astype(jnp.int32).reshape(N_DP, ROWS_DEV), row_weight.reshape(N_DP, ROWS_DEV), whitened.reshape(N_DP, ROWS_DEV))
    start = (jnp.zeros((COEFFS, COEFFS), jnp.float32), jnp.zeros((COEFFS,), jnp.float32))
    (normal, gradient), unused = lax.scan(accumulate, start, blocks)
    halves = N_COEF // 2
    tiles = []
    for panel_index in range(N_COEF):
        panel_rows = normal[panel_index * PAN:(panel_index + 1) * PAN]
        pieces = []
        for offset in range(halves + 1):
            other_index = (panel_index + offset) % N_COEF
            pieces.append(panel_rows[:, other_index * PAN:(other_index + 1) * PAN])
        tiles.append(jnp.concatenate(pieces, axis=1))
    gram_band = jnp.stack(tiles)
    return (gram_band, gradient.reshape(N_COEF, PAN))
```

```python
import math

import jax
import jax.numpy as jnp
from jax import lax
from jax.sharding import PartitionSpec as P

GROUPS = ((0, 1, 2), (3, 4))


def from_ahead(value, steps):
    count = lax.axis_size("coef")
    pairs = [((target + steps) % count, target) for target in range(count)]
    return lax.ppermute(value, "coef", pairs)


def swap(value, bit):
    count = lax.axis_size("dp")
    return lax.ppermute(value, "dp", [(source, source ^ bit) for source in range(count)])


def picked(table, index):
    hot = (index[:, None] == lax.broadcasted_iota(jnp.int32, (1, table.shape[0]), 1))
    return lax.dot_general(
        hot.astype(jnp.bfloat16), table, (((1,), (0,)), ((), ())),
        preferred_element_type=jnp.float32,
    )


def cross(left_panel, right_panel):
    return lax.dot_general(
        left_panel, right_panel, (((0,), (0,)), ((), ())), preferred_element_type=jnp.float32
    )


def scattered(keep, give, travel):
    count = lax.axis_size("dp")
    bit = 1
    while True:
        sent = [g.astype(t) for g, t in zip(give, travel)]
        if len(sent) > 1:
            sent = lax.optimization_barrier(sent)
        total = [k + swap(g, bit).astype(jnp.float32) for k, g in zip(keep, sent)]
        bit *= 2
        if bit == count:
            return total
        half = total[0].shape[0] // 2
        keep, give = [t[:half] for t in total], [t[half:] for t in total]


def local(location, component, epoch_bin, residual, row_scale, spatial_table, spline_table):
    dp = lax.axis_size("dp")
    me = lax.axis_index("dp")
    total_rows = location.shape[0] * dp
    scale = row_scale.astype(jnp.float32)
    row_weight = scale * (1.0 / math.sqrt(total_rows))
    own = (
        picked(spatial_table, 3 * location + component)
        * picked(spline_table, epoch_bin)
        * row_weight[:, None]
    ).astype(jnp.bfloat16)
    whitened = (scale * residual.astype(jnp.float32)).astype(jnp.bfloat16)

    panels = [own] + [from_ahead(own, k) for k in range(1, lax.axis_size("coef") // 2 + 1)]

    size = own.shape[1]
    each = size // dp
    place = lax.broadcasted_iota(jnp.int32, (1, size), 1)
    block, inner = place // each, place % each
    mirrored = jnp.zeros_like(block)
    bits = dp.bit_length() - 1
    for b in range(bits):
        mirrored = mirrored | (((block >> b) & 1) << (bits - 1 - b))
    wanted = each * (me ^ mirrored) + inner
    order = (lax.broadcasted_iota(jnp.int32, (size, 1), 0) == wanted).astype(jnp.bfloat16)
    left = lax.dot_general(
        own, order, (((1,), (0,)), ((), ())), preferred_element_type=jnp.float32
    ).astype(jnp.bfloat16)
    kept, given = left[:, : size // 2], left[:, size // 2 :]

    pieces = []
    given_piece = None
    for group in GROUPS:
        parts = [panels[k] for k in group]
        travel = [jnp.bfloat16]
        if given_piece is not None:
            parts, _ = lax.optimization_barrier((parts, given_piece))
        right = jnp.concatenate(parts, axis=1)
        given_piece = cross(given, right).astype(jnp.bfloat16)
        keep, give = [cross(kept, right)], [given_piece]
        if not pieces:
            keep.append(cross(kept, whitened))
            give.append(cross(given, whitened))
            travel.append(jnp.float32)
        total = scattered(keep, give, travel)
        pieces.append(total[0])
        if len(total) > 1:
            gradient = total[1]
    gram_band = jnp.concatenate(pieces, axis=1)
    return (gram_band[None], gradient[None])


def solution(mesh):
    return jax.shard_map(
        local,
        mesh=mesh,
        in_specs=(P("dp"), P("dp"), P("dp"), P("dp"), P("dp"), P(None, "coef"), P(None, "coef")),
        out_specs=(P("coef", "dp", None), P("coef", "dp")),
        check_vma=False,
    )
```

```python
import functools
import math

import jax
import jax.numpy as jnp
from jax import lax
from jax.experimental import pallas as pl
from jax.experimental.pallas import tpu as pltpu
from jax.sharding import PartitionSpec as P

ORDERS = (((1, 2), (2, 2), (4, 4), (16, 4)), ((1, 2), (4, 4), (16, 4), (2, 2)))
GROUPS = ((0, 1, 2), (3, 4))
LANES = 128
MESH = pl.DeviceIdType.MESH


def picked(table, index):
    hot = (index[:, None] == lax.broadcasted_iota(jnp.int32, (1, table.shape[0]), 1))
    return lax.dot_general(
        hot.astype(jnp.bfloat16), table, (((1,), (0,)), ((), ())),
        preferred_element_type=jnp.float32,
    )


def partner(me, unit, choice):
    low = lax.rem(me // unit, 2)
    high = lax.rem(me // (2 * unit), 2)
    return me + (choice % 2) * unit * (1 - 2 * low) + (choice // 2) * 2 * unit * (1 - 2 * high)


def ordered(own, me, order):
    size = own.shape[1]
    blocks = math.prod(radix for _, radix in order)
    each = size // blocks
    place = lax.broadcasted_iota(jnp.int32, (1, size), 1)
    rest, inner = place // each, place % each
    mask = jnp.zeros_like(rest)
    for unit, radix in reversed(order):
        mask = mask + unit * (rest % radix)
        rest = rest // radix
    wanted = each * (me ^ mask) + inner
    hot = (lax.broadcasted_iota(jnp.int32, (size, 1), 0) == wanted).astype(jnp.bfloat16)
    return lax.dot_general(
        hot, own, (((0,), (1,)), ((), ())), preferred_element_type=jnp.float32
    ).astype(jnp.bfloat16)


def band_kernel(dp, coef, own_ref, left_a, left_b, slope_ref, band_ref, gradient_ref, *scratch):
    panels, send_a, send_b = scratch[0], scratch[1:5], scratch[5:9]
    recv_a, recv_b = scratch[9:13], scratch[13:17]
    panel_send, panel_recv, sum_send, sum_recv = scratch[17:21]
    me, mine = lax.axis_index("dp"), lax.axis_index("coef")
    pan = own_ref.shape[1]

    barrier = pltpu.get_barrier_semaphore()
    friends = [(me, lax.rem(mine + k, coef)) for k in range(1, coef)]
    friends += [(partner(me, u, q), mine) for u, r in ORDERS[0] for q in range(1, r)]
    for friend in friends:
        pl.semaphore_signal(barrier, inc=1, device_id=friend, device_id_type=MESH)
    pl.semaphore_wait(barrier, len(friends))

    fetches = []
    for k in range(1, coef // 2 + 1):
        fetch = pltpu.make_async_remote_copy(
            src_ref=own_ref,
            dst_ref=panels.at[k - 1],
            send_sem=panel_send.at[k - 1],
            recv_sem=panel_recv.at[k - 1],
            device_id=(me, lax.rem(mine + coef - k, coef)),
            device_id_type=MESH,
        )
        fetch.start()
        fetches.append(fetch)

    def packed(gram, slope):
        high = slope.astype(jnp.bfloat16).astype(jnp.float32)
        rest = slope - high
        middle = rest.astype(jnp.bfloat16).astype(jnp.float32)
        lane = lax.broadcasted_iota(jnp.int32, slope.shape, 1)
        three = jnp.where(lane == 0, high, jnp.where(lane == 1, middle, rest - middle))
        three = jnp.where(lane < 3, three, 0.0)
        return gram.astype(jnp.bfloat16), three.astype(jnp.bfloat16)

    def start(group, stage, values):
        unit, radix = ORDERS[group][stage]
        send, recv = (send_a, send_b)[group][stage], (recv_a, recv_b)[group][stage]
        chunk = values[0].shape[0] // radix
        copies = []
        for q in range(1, radix):
            cut = [v[q * chunk : (q + 1) * chunk] for v in values]
            if len(cut) == 2:
                gram, three = packed(*cut)
                width = gram.shape[1]
                send[q - 1, :, :width] = gram
                send[q - 1, :, width:] = three
            else:
                send[q - 1] = cut[0].astype(jnp.bfloat16)
            copy = pltpu.make_async_remote_copy(
                src_ref=send.at[q - 1],
                dst_ref=recv.at[q - 1],
                send_sem=sum_send.at[group, stage, q - 1],
                recv_sem=sum_recv.at[group, stage, q - 1],
                device_id=(partner(me, unit, q), mine),
                device_id_type=MESH,
            )
            copy.start()
            copies.append(copy)
        return copies, [v[:chunk] for v in values], recv

    def finish(state):
        copies, values, recv = state
        for q, copy in enumerate(copies):
            copy.wait()
            got = recv[q].astype(jnp.float32)
            width = values[0].shape[1]
            values = [values[0] + got[:, :width]] + [
                v + jnp.sum(got[:, width:], axis=1, keepdims=True) for v in values[1:]
            ]
        return values

    def product(left, k):
        right = own_ref[...] if k == 0 else panels[k - 1]
        return jnp.dot(left[...], right, preferred_element_type=jnp.float32)

    blocks = [product(left_a, 0)]
    for k in GROUPS[0][1:]:
        fetches[k - 1].wait()
        blocks.append(product(left_a, k))
    state_a = start(0, 0, [jnp.concatenate(blocks, axis=1), slope_ref[...]])
    blocks = []
    for k in GROUPS[1]:
        fetches[k - 1].wait()
        blocks.append(product(left_b, k))
    state_b = start(1, 0, [jnp.concatenate(blocks, axis=1)])
    for stage in range(1, len(ORDERS[0])):
        state_a = start(0, stage, finish(state_a))
        state_b = start(1, stage, finish(state_b))
    gram, slope = finish(state_a)
    band_ref[:, : gram.shape[1]] = gram
    gradient_ref[...] = slope
    band_ref[:, gram.shape[1] :] = finish(state_b)[0]


def band(own, left_a, left_b, slope):
    dp, coef = lax.axis_size("dp"), lax.axis_size("coef")
    rows, pan = own.shape
    widths = [len(GROUPS[0]) * pan + LANES, len(GROUPS[1]) * pan]
    buffers = []
    for order, width in zip(ORDERS, widths):
        left = pan
        for _, radix in order:
            left //= radix
            buffers.append(pltpu.VMEM((radix - 1, left, width), jnp.bfloat16))
    each = pan // dp
    vmem = pl.BlockSpec(memory_space=pltpu.VMEM)
    return pl.pallas_call(
        functools.partial(band_kernel, dp, coef),
        out_shape=(
            jax.ShapeDtypeStruct((each, (coef // 2 + 1) * pan), jnp.float32),
            jax.ShapeDtypeStruct((each, LANES), jnp.float32),
        ),
        in_specs=[vmem] * 4,
        out_specs=(vmem, vmem),
        scratch_shapes=[pltpu.VMEM((coef // 2, rows, pan), jnp.bfloat16)]
        + buffers
        + buffers
        + [
            pltpu.SemaphoreType.DMA((coef // 2,)),
            pltpu.SemaphoreType.DMA((coef // 2,)),
            pltpu.SemaphoreType.DMA((2, 4, 3)),
            pltpu.SemaphoreType.DMA((2, 4, 3)),
        ],
        compiler_params=pltpu.CompilerParams(
            collective_id=0, has_side_effects=True, vmem_limit_bytes=48 * 1024 * 1024
        ),
    )(own, left_a, left_b, slope)


def local(location, component, epoch_bin, residual, row_scale, spatial_table, spline_table):
    dp = lax.axis_size("dp")
    me = lax.axis_index("dp")
    total_rows = location.shape[0] * dp
    scale = row_scale.astype(jnp.float32)
    row_weight = scale * (1.0 / math.sqrt(total_rows))
    own = (
        picked(spatial_table, 3 * location + component)
        * picked(spline_table, epoch_bin)
        * row_weight[:, None]
    ).astype(jnp.bfloat16)
    whitened = (scale * residual.astype(jnp.float32)).astype(jnp.bfloat16)

    left_a, left_b = (ordered(own, me, order) for order in ORDERS)
    slope = lax.dot_general(
        left_a, whitened, (((1,), (0,)), ((), ())), preferred_element_type=jnp.float32
    )
    slope = jnp.broadcast_to(slope[:, None], (slope.shape[0], LANES))
    gram_band, gradient = band(own, left_a, left_b, slope)
    return (gram_band[None], gradient[None, :, 0])


def solution(mesh):
    return jax.shard_map(
        local,
        mesh=mesh,
        in_specs=(P("dp"), P("dp"), P("dp"), P("dp"), P("dp"), P(None, "coef"), P(None, "coef")),
        out_specs=(P("coef", "dp", None), P("coef", "dp")),
        check_vma=False,
    )
```

```python
import functools
import math

import jax
import jax.numpy as jnp
from jax import lax
from jax.experimental import pallas as pl
from jax.experimental.pallas import tpu as pltpu
from jax.sharding import PartitionSpec as P

ORDERS = (((1, 2), (2, 2), (4, 4), (16, 4)), ((1, 2), (4, 4), (16, 4), (2, 2)))
WAY = (0, 1, 0, 1, 0)
LANES = 128
MESH = pl.DeviceIdType.MESH


def picked(table, index):
    hot = (index[:, None] == lax.broadcasted_iota(jnp.int32, (1, table.shape[0]), 1))
    return lax.dot_general(
        hot.astype(jnp.bfloat16), table, (((1,), (0,)), ((), ())),
        preferred_element_type=jnp.float32,
    )


def partner(me, unit, choice):
    low = lax.rem(me // unit, 2)
    high = lax.rem(me // (2 * unit), 2)
    return me + (choice % 2) * unit * (1 - 2 * low) + (choice // 2) * 2 * unit * (1 - 2 * high)


def ordered(own, me, order):
    size = own.shape[1]
    blocks = math.prod(radix for _, radix in order)
    each = size // blocks
    place = lax.broadcasted_iota(jnp.int32, (1, size), 1)
    rest, inner = place // each, place % each
    mask = jnp.zeros_like(rest)
    for unit, radix in reversed(order):
        mask = mask + unit * (rest % radix)
        rest = rest // radix
    wanted = each * (me ^ mask) + inner
    hot = (lax.broadcasted_iota(jnp.int32, (size, 1), 0) == wanted).astype(jnp.bfloat16)
    return lax.dot_general(
        hot, own, (((0,), (1,)), ((), ())), preferred_element_type=jnp.float32
    ).astype(jnp.bfloat16)


def band_kernel(dp, coef, own_ref, left_a, left_b, slope_ref, band_ref, gradient_ref, *scratch):
    panels = scratch[0]
    stages, count = len(ORDERS[0]), len(WAY)
    sends = [scratch[1 + g * stages : 1 + (g + 1) * stages] for g in range(count)]
    recvs = [scratch[1 + (count + g) * stages : 1 + (count + g + 1) * stages] for g in range(count)]
    panel_send, panel_recv, sum_send, sum_recv = scratch[1 + 2 * count * stages :]
    me, mine = lax.axis_index("dp"), lax.axis_index("coef")
    pan = own_ref.shape[1]

    barrier = pltpu.get_barrier_semaphore()
    friends = [(me, lax.rem(mine + k, coef)) for k in range(1, coef)]
    friends += [(partner(me, u, q), mine) for u, r in ORDERS[0] for q in range(1, r)]
    for friend in friends:
        pl.semaphore_signal(barrier, inc=1, device_id=friend, device_id_type=MESH)
    pl.semaphore_wait(barrier, len(friends))

    fetches = []
    for k in range(1, coef // 2 + 1):
        fetch = pltpu.make_async_remote_copy(
            src_ref=own_ref,
            dst_ref=panels.at[k - 1],
            send_sem=panel_send.at[k - 1],
            recv_sem=panel_recv.at[k - 1],
            device_id=(me, lax.rem(mine + coef - k, coef)),
            device_id_type=MESH,
        )
        fetch.start()
        fetches.append(fetch)

    def packed(gram, slope):
        high = slope.astype(jnp.bfloat16).astype(jnp.float32)
        rest = slope - high
        middle = rest.astype(jnp.bfloat16).astype(jnp.float32)
        lane = lax.broadcasted_iota(jnp.int32, slope.shape, 1)
        three = jnp.where(lane == 0, high, jnp.where(lane == 1, middle, rest - middle))
        three = jnp.where(lane < 3, three, 0.0)
        return gram.astype(jnp.bfloat16), three.astype(jnp.bfloat16)

    def start(group, stage, values):
        unit, radix = ORDERS[WAY[group]][stage]
        send, recv = sends[group][stage], recvs[group][stage]
        chunk = values[0].shape[0] // radix
        copies = []
        for q in range(1, radix):
            cut = [v[q * chunk : (q + 1) * chunk] for v in values]
            if len(cut) == 2:
                gram, three = packed(*cut)
                width = gram.shape[1]
                send[q - 1, :, :width] = gram
                send[q - 1, :, width:] = three
            else:
                send[q - 1] = cut[0].astype(jnp.bfloat16)
            copy = pltpu.make_async_remote_copy(
                src_ref=send.at[q - 1],
                dst_ref=recv.at[q - 1],
                send_sem=sum_send.at[group, stage, q - 1],
                recv_sem=sum_recv.at[group, stage, q - 1],
                device_id=(partner(me, unit, q), mine),
                device_id_type=MESH,
            )
            copy.start()
            copies.append(copy)
        return copies, [v[:chunk] for v in values], recv

    def finish(state):
        copies, values, recv = state
        for q, copy in enumerate(copies):
            copy.wait()
            got = recv[q].astype(jnp.float32)
            width = values[0].shape[1]
            values = [values[0] + got[:, :width]] + [
                v + jnp.sum(got[:, width:], axis=1, keepdims=True) for v in values[1:]
            ]
        return values

    def product(k):
        left = (left_a, left_b)[WAY[k]]
        right = own_ref[...] if k == 0 else panels[k - 1]
        return jnp.dot(left[...], right, preferred_element_type=jnp.float32)

    state = [None] * count
    for wave in range(count + stages):
        for k in range(count):
            stage = wave - k
            if stage == 0:
                if k > 0:
                    fetches[k - 1].wait()
                values = [product(k)] + ([slope_ref[...]] if k == 0 else [])
                state[k] = start(k, 0, values)
            elif 0 < stage < stages:
                state[k] = start(k, stage, finish(state[k]))
            elif stage == stages:
                values = finish(state[k])
                band_ref[:, k * pan : (k + 1) * pan] = values[0]
                if k == 0:
                    gradient_ref[...] = values[1]


def band(own, left_a, left_b, slope):
    dp, coef = lax.axis_size("dp"), lax.axis_size("coef")
    rows, pan = own.shape
    buffers = []
    for k, way in enumerate(WAY):
        left = pan
        width = pan + LANES if k == 0 else pan
        for _, radix in ORDERS[way]:
            left //= radix
            buffers.append(pltpu.VMEM((radix - 1, left, width), jnp.bfloat16))
    each = pan // dp
    vmem = pl.BlockSpec(memory_space=pltpu.VMEM)
    return pl.pallas_call(
        functools.partial(band_kernel, dp, coef),
        out_shape=(
            jax.ShapeDtypeStruct((each, (coef // 2 + 1) * pan), jnp.float32),
            jax.ShapeDtypeStruct((each, LANES), jnp.float32),
        ),
        in_specs=[vmem] * 4,
        out_specs=(vmem, vmem),
        scratch_shapes=[pltpu.VMEM((coef // 2, rows, pan), jnp.bfloat16)]
        + buffers
        + buffers
        + [
            pltpu.SemaphoreType.DMA((coef // 2,)),
            pltpu.SemaphoreType.DMA((coef // 2,)),
            pltpu.SemaphoreType.DMA((len(WAY), 4, 3)),
            pltpu.SemaphoreType.DMA((len(WAY), 4, 3)),
        ],
        compiler_params=pltpu.CompilerParams(
            collective_id=0, has_side_effects=True, vmem_limit_bytes=48 * 1024 * 1024
        ),
    )(own, left_a, left_b, slope)


def local(location, component, epoch_bin, residual, row_scale, spatial_table, spline_table):
    dp = lax.axis_size("dp")
    me = lax.axis_index("dp")
    total_rows = location.shape[0] * dp
    scale = row_scale.astype(jnp.float32)
    row_weight = scale * (1.0 / math.sqrt(total_rows))
    own = (
        picked(spatial_table, 3 * location + component)
        * picked(spline_table, epoch_bin)
        * row_weight[:, None]
    ).astype(jnp.bfloat16)
    whitened = (scale * residual.astype(jnp.float32)).astype(jnp.bfloat16)

    left_a, left_b = (ordered(own, me, order) for order in ORDERS)
    slope = lax.dot_general(
        left_a, whitened, (((1,), (0,)), ((), ())), preferred_element_type=jnp.float32
    )
    slope = jnp.broadcast_to(slope[:, None], (slope.shape[0], LANES))
    gram_band, gradient = band(own, left_a, left_b, slope)
    return (gram_band[None], gradient[None, :, 0])


def solution(mesh):
    return jax.shard_map(
        local,
        mesh=mesh,
        in_specs=(P("dp"), P("dp"), P("dp"), P("dp"), P("dp"), P(None, "coef"), P(None, "coef")),
        out_specs=(P("coef", "dp", None), P("coef", "dp")),
        check_vma=False,
    )
```

```python
import functools
import math

import jax
import jax.numpy as jnp
from jax import lax
from jax.experimental import pallas as pl
from jax.experimental.pallas import tpu as pltpu
from jax.sharding import PartitionSpec as P

ORDERS = (((1, 2), (2, 2), (4, 4), (16, 4)), ((1, 2), (4, 4), (16, 4), (2, 2)))
WAY = (0, 1, 0, 1, 0)
LANES = 128
MESH = pl.DeviceIdType.MESH


def picked(table, index):
    hot = (index[:, None] == lax.broadcasted_iota(jnp.int32, (1, table.shape[0]), 1))
    return lax.dot_general(
        hot.astype(jnp.bfloat16), table, (((1,), (0,)), ((), ())),
        preferred_element_type=jnp.float32,
    )


def partner(me, unit, choice):
    low = lax.rem(me // unit, 2)
    high = lax.rem(me // (2 * unit), 2)
    return me + (choice % 2) * unit * (1 - 2 * low) + (choice // 2) * 2 * unit * (1 - 2 * high)


def ordered(own, me, order):
    size = own.shape[1]
    blocks = math.prod(radix for _, radix in order)
    each = size // blocks
    place = lax.broadcasted_iota(jnp.int32, (1, size), 1)
    rest, inner = place // each, place % each
    mask = jnp.zeros_like(rest)
    for unit, radix in reversed(order):
        mask = mask + unit * (rest % radix)
        rest = rest // radix
    wanted = each * (me ^ mask) + inner
    hot = (lax.broadcasted_iota(jnp.int32, (size, 1), 0) == wanted).astype(jnp.bfloat16)
    return lax.dot_general(
        hot, own, (((0,), (1,)), ((), ())), preferred_element_type=jnp.float32
    ).astype(jnp.bfloat16)


def band_kernel(dp, coef, own_ref, left_a, left_b, slope_ref, band_ref, gradient_ref, *scratch):
    panels = scratch[0]
    stages, count = len(ORDERS[0]), len(WAY)
    sends = [scratch[1 + g * stages : 1 + (g + 1) * stages] for g in range(count)]
    recvs = [scratch[1 + (count + g) * stages : 1 + (count + g + 1) * stages] for g in range(count)]
    panel_send, panel_recv, sum_send, sum_recv = scratch[1 + 2 * count * stages :]
    me, mine = lax.axis_index("dp"), lax.axis_index("coef")
    pan = own_ref.shape[1]

    barrier = pltpu.get_barrier_semaphore()
    friends = [(me, lax.rem(mine + k, coef)) for k in range(1, coef)]
    friends += [(partner(me, u, q), mine) for u, r in ORDERS[0] for q in range(1, r)]
    for friend in friends:
        pl.semaphore_signal(barrier, inc=1, device_id=friend, device_id_type=MESH)
    pl.semaphore_wait(barrier, len(friends))

    x = lax.rem(mine, 2)
    back, beside = (me, lax.rem(mine + coef - 2, coef)), (me, mine + 1 - 2 * x)
    offsets = [0, 2, 3 - 2 * x, 4, 1 + 2 * x]
    half = own_ref.shape[0] // 2

    def pass_on(source, slot, part, target):
        rows = pl.ds(part * half, half)
        return pltpu.make_async_remote_copy(
            src_ref=own_ref.at[rows] if source is None else panels.at[source, rows],
            dst_ref=panels.at[slot, rows],
            send_sem=panel_send.at[slot, part],
            recv_sem=panel_recv.at[slot, part],
            device_id=target,
            device_id_type=MESH,
        )

    near = [pass_on(None, 0, part, back) for part in range(2)]
    across = [pass_on(0, 1, part, beside) for part in range(2)]
    far = [pass_on(0, 2, part, back) for part in range(2)]
    last_one = [pass_on(None, 3, part, beside) for part in range(2)]
    last_zero = [pass_on(2, 3, part, beside) for part in range(2)]

    def when_x(value, action):
        @pl.when(x == value)
        def _():
            action()

    for part in range(2):
        near[part].start()
    for part in range(2):
        when_x(1, last_one[part].start)

    def arrive(slot):
        for part in range(2):
            if slot == 0:
                near[part].wait_recv()
                far[part].start()
                across[part].start()
            elif slot == 1:
                across[part].wait_recv()
            elif slot == 2:
                far[part].wait_recv()
                when_x(0, last_zero[part].start)
            else:
                last_one[part].wait_recv()

    def packed(gram, slope):
        high = slope.astype(jnp.bfloat16).astype(jnp.float32)
        rest = slope - high
        middle = rest.astype(jnp.bfloat16).astype(jnp.float32)
        lane = lax.broadcasted_iota(jnp.int32, slope.shape, 1)
        three = jnp.where(lane == 0, high, jnp.where(lane == 1, middle, rest - middle))
        three = jnp.where(lane < 3, three, 0.0)
        return gram.astype(jnp.bfloat16), three.astype(jnp.bfloat16)

    def start(group, stage, values):
        unit, radix = ORDERS[WAY[group]][stage]
        send, recv = sends[group][stage], recvs[group][stage]
        chunk = values[0].shape[0] // radix
        copies = []
        for q in range(1, radix):
            cut = [v[q * chunk : (q + 1) * chunk] for v in values]
            if len(cut) == 2:
                gram, three = packed(*cut)
                width = gram.shape[1]
                send[q - 1, :, :width] = gram
                send[q - 1, :, width:] = three
            else:
                send[q - 1] = cut[0].astype(jnp.bfloat16)
            copy = pltpu.make_async_remote_copy(
                src_ref=send.at[q - 1],
                dst_ref=recv.at[q - 1],
                send_sem=sum_send.at[group, stage, q - 1],
                recv_sem=sum_recv.at[group, stage, q - 1],
                device_id=(partner(me, unit, q), mine),
                device_id_type=MESH,
            )
            copy.start()
            copies.append(copy)
        return copies, [v[:chunk] for v in values], recv

    def finish(state):
        copies, values, recv = state
        for q, copy in enumerate(copies):
            copy.wait()
            got = recv[q].astype(jnp.float32)
            width = values[0].shape[1]
            values = [values[0] + got[:, :width]] + [
                v + jnp.sum(got[:, width:], axis=1, keepdims=True) for v in values[1:]
            ]
        return values

    def product(k):
        left = (left_a, left_b)[WAY[k]]
        right = own_ref[...] if k == 0 else panels[k - 1]
        return jnp.dot(left[...], right, preferred_element_type=jnp.float32)

    state = [None] * count
    for wave in range(count + stages):
        for k in range(count):
            stage = wave - k
            if stage == 0:
                if k > 0:
                    arrive(k - 1)
                values = [product(k)] + ([slope_ref[...]] if k == 0 else [])
                state[k] = start(k, 0, values)
            elif 0 < stage < stages:
                state[k] = start(k, stage, finish(state[k]))
            elif stage == stages:
                values = finish(state[k])
                column = offsets[k] * pan
                if k in (2, 4):
                    column = pl.multiple_of(column, LANES)
                band_ref[:, pl.ds(column, pan)] = values[0]
                if k == 0:
                    gradient_ref[...] = values[1]
    for part in range(2):
        near[part].wait_send()
        across[part].wait_send()
        far[part].wait_send()
        when_x(1, last_one[part].wait_send)
        when_x(0, last_zero[part].wait_send)


def band(own, left_a, left_b, slope):
    dp, coef = lax.axis_size("dp"), lax.axis_size("coef")
    rows, pan = own.shape
    buffers = []
    for k, way in enumerate(WAY):
        left = pan
        width = pan + LANES if k == 0 else pan
        for _, radix in ORDERS[way]:
            left //= radix
            buffers.append(pltpu.VMEM((radix - 1, left, width), jnp.bfloat16))
    each = pan // dp
    vmem = pl.BlockSpec(memory_space=pltpu.VMEM)
    return pl.pallas_call(
        functools.partial(band_kernel, dp, coef),
        out_shape=(
            jax.ShapeDtypeStruct((each, (coef // 2 + 1) * pan), jnp.float32),
            jax.ShapeDtypeStruct((each, LANES), jnp.float32),
        ),
        in_specs=[vmem] * 4,
        out_specs=(vmem, vmem),
        scratch_shapes=[pltpu.VMEM((coef // 2, rows, pan), jnp.bfloat16)]
        + buffers
        + buffers
        + [
            pltpu.SemaphoreType.DMA((coef // 2, 2)),
            pltpu.SemaphoreType.DMA((coef // 2, 2)),
            pltpu.SemaphoreType.DMA((len(WAY), 4, 3)),
            pltpu.SemaphoreType.DMA((len(WAY), 4, 3)),
        ],
        compiler_params=pltpu.CompilerParams(
            collective_id=0, has_side_effects=True, vmem_limit_bytes=48 * 1024 * 1024
        ),
    )(own, left_a, left_b, slope)


def local(location, component, epoch_bin, residual, row_scale, spatial_table, spline_table):
    dp = lax.axis_size("dp")
    me = lax.axis_index("dp")
    total_rows = location.shape[0] * dp
    scale = row_scale.astype(jnp.float32)
    row_weight = scale * (1.0 / math.sqrt(total_rows))
    own = (
        picked(spatial_table, 3 * location + component)
        * picked(spline_table, epoch_bin)
        * row_weight[:, None]
    ).astype(jnp.bfloat16)
    whitened = (scale * residual.astype(jnp.float32)).astype(jnp.bfloat16)

    left_a, left_b = (ordered(own, me, order) for order in ORDERS)
    slope = lax.dot_general(
        left_a, whitened, (((1,), (0,)), ((), ())), preferred_element_type=jnp.float32
    )
    slope = jnp.broadcast_to(slope[:, None], (slope.shape[0], LANES))
    gram_band, gradient = band(own, left_a, left_b, slope)
    return (gram_band[None], gradient[None, :, 0])


def solution(mesh):
    return jax.shard_map(
        local,
        mesh=mesh,
        in_specs=(P("dp"), P("dp"), P("dp"), P("dp"), P("dp"), P(None, "coef"), P(None, "coef")),
        out_specs=(P("coef", "dp", None), P("coef", "dp")),
        check_vma=False,
    )
```

```python
import functools
import math

import jax
import jax.numpy as jnp
from jax import lax
from jax.experimental import pallas as pl
from jax.experimental.pallas import tpu as pltpu
from jax.sharding import PartitionSpec as P

ORDERS = (((1, 2), (4, 4), (16, 4), (2, 2)),) * 2
WAY = (0, 1, 0, 1, 0)
LANES = 128
MESH = pl.DeviceIdType.MESH


def picked(table, index):
    hot = (index[:, None] == lax.broadcasted_iota(jnp.int32, (1, table.shape[0]), 1))
    return lax.dot_general(
        hot.astype(jnp.bfloat16), table, (((1,), (0,)), ((), ())),
        preferred_element_type=jnp.float32,
    )


def partner(me, unit, choice):
    low = lax.rem(me // unit, 2)
    high = lax.rem(me // (2 * unit), 2)
    return me + (choice % 2) * unit * (1 - 2 * low) + (choice // 2) * 2 * unit * (1 - 2 * high)


def ordered(own, me, order):
    size = own.shape[1]
    blocks = math.prod(radix for _, radix in order)
    each = size // blocks
    place = lax.broadcasted_iota(jnp.int32, (1, size), 1)
    rest, inner = place // each, place % each
    mask = jnp.zeros_like(rest)
    for unit, radix in reversed(order):
        mask = mask + unit * (rest % radix)
        rest = rest // radix
    wanted = each * (me ^ mask) + inner
    hot = (lax.broadcasted_iota(jnp.int32, (size, 1), 0) == wanted).astype(jnp.bfloat16)
    return lax.dot_general(
        hot, own, (((0,), (1,)), ((), ())), preferred_element_type=jnp.float32
    ).astype(jnp.bfloat16)


def band_kernel(dp, coef, own_ref, left_a, left_b, slope_ref, band_ref, gradient_ref, *scratch):
    panels = scratch[0]
    stages, count = len(ORDERS[0]), len(WAY)
    sends = [scratch[1 + g * stages : 1 + (g + 1) * stages] for g in range(count)]
    recvs = [scratch[1 + (count + g) * stages : 1 + (count + g + 1) * stages] for g in range(count)]
    panel_send, panel_recv, sum_send, sum_recv = scratch[1 + 2 * count * stages :]
    me, mine = lax.axis_index("dp"), lax.axis_index("coef")
    pan = own_ref.shape[1]

    barrier = pltpu.get_barrier_semaphore()
    friends = [(me, lax.rem(mine + k, coef)) for k in range(1, coef)]
    friends += [(partner(me, u, q), mine) for u, r in ORDERS[0] for q in range(1, r)]
    for friend in friends:
        pl.semaphore_signal(barrier, inc=1, device_id=friend, device_id_type=MESH)
    pl.semaphore_wait(barrier, len(friends))

    x = lax.rem(mine, 2)
    back, beside = (me, lax.rem(mine + coef - 2, coef)), (me, mine + 1 - 2 * x)
    offsets = [0, 2, 3 - 2 * x, 4, 1 + 2 * x]
    half = own_ref.shape[0] // 2

    def pass_on(source, slot, part, target):
        rows = pl.ds(part * half, half)
        return pltpu.make_async_remote_copy(
            src_ref=own_ref.at[rows] if source is None else panels.at[source, rows],
            dst_ref=panels.at[slot, rows],
            send_sem=panel_send.at[slot, part],
            recv_sem=panel_recv.at[slot, part],
            device_id=target,
            device_id_type=MESH,
        )

    near = [pass_on(None, 0, part, back) for part in range(2)]
    across = [pass_on(0, 1, part, beside) for part in range(2)]
    far = [pass_on(0, 2, part, back) for part in range(2)]
    last_one = [pass_on(None, 3, part, beside) for part in range(2)]
    last_zero = [pass_on(2, 3, part, beside) for part in range(2)]

    def when_x(value, action):
        @pl.when(x == value)
        def _():
            action()

    for part in range(2):
        near[part].start()
    for part in range(2):
        when_x(1, last_one[part].start)

    def arrive(slot):
        for part in range(2):
            if slot == 0:
                near[part].wait_recv()
                far[part].start()
                across[part].start()
            elif slot == 1:
                across[part].wait_recv()
            elif slot == 2:
                far[part].wait_recv()
                when_x(0, last_zero[part].start)
            else:
                last_one[part].wait_recv()

    def packed(gram, slope):
        high = slope.astype(jnp.bfloat16).astype(jnp.float32)
        rest = slope - high
        middle = rest.astype(jnp.bfloat16).astype(jnp.float32)
        lane = lax.broadcasted_iota(jnp.int32, slope.shape, 1)
        three = jnp.where(lane == 0, high, jnp.where(lane == 1, middle, rest - middle))
        three = jnp.where(lane < 3, three, 0.0)
        return gram.astype(jnp.bfloat16), three.astype(jnp.bfloat16)

    def start(group, stage, values):
        unit, radix = ORDERS[WAY[group]][stage]
        send, recv = sends[group][stage], recvs[group][stage]
        chunk = values[0].shape[0] // radix
        copies = []
        for q in range(1, radix):
            cut = [v[q * chunk : (q + 1) * chunk] for v in values]
            if len(cut) == 2:
                gram, three = packed(*cut)
                width = gram.shape[1]
                send[q - 1, :, :width] = gram
                send[q - 1, :, width:] = three
            else:
                send[q - 1] = cut[0].astype(jnp.bfloat16)
            copy = pltpu.make_async_remote_copy(
                src_ref=send.at[q - 1],
                dst_ref=recv.at[q - 1],
                send_sem=sum_send.at[group, stage, q - 1],
                recv_sem=sum_recv.at[group, stage, q - 1],
                device_id=(partner(me, unit, q), mine),
                device_id_type=MESH,
            )
            copy.start()
            copies.append(copy)
        return copies, [v[:chunk] for v in values], recv

    def finish(state):
        copies, values, recv = state
        for q, copy in enumerate(copies):
            copy.wait()
            got = recv[q].astype(jnp.float32)
            width = values[0].shape[1]
            values = [values[0] + got[:, :width]] + [
                v + jnp.sum(got[:, width:], axis=1, keepdims=True) for v in values[1:]
            ]
        return values

    def product(k):
        left = (left_a, left_b)[WAY[k]]
        right = own_ref[...] if k == 0 else panels[k - 1]
        return jnp.dot(left[...], right, preferred_element_type=jnp.float32)

    state = [None] * count
    for wave in range(count + stages):
        for k in reversed(range(count)):
            stage = wave - k
            if stage == 0:
                if k > 0:
                    arrive(k - 1)
                values = [product(k)] + ([slope_ref[...]] if k == 0 else [])
                state[k] = start(k, 0, values)
            elif 0 < stage < stages:
                state[k] = start(k, stage, finish(state[k]))
            elif stage == stages:
                values = finish(state[k])
                column = offsets[k] * pan
                if k in (2, 4):
                    column = pl.multiple_of(column, LANES)
                band_ref[:, pl.ds(column, pan)] = values[0]
                if k == 0:
                    gradient_ref[...] = values[1]
    for part in range(2):
        near[part].wait_send()
        across[part].wait_send()
        far[part].wait_send()
        when_x(1, last_one[part].wait_send)
        when_x(0, last_zero[part].wait_send)


def band(own, left_a, left_b, slope):
    dp, coef = lax.axis_size("dp"), lax.axis_size("coef")
    rows, pan = own.shape
    buffers = []
    for k, way in enumerate(WAY):
        left = pan
        width = pan + LANES if k == 0 else pan
        for _, radix in ORDERS[way]:
            left //= radix
            buffers.append(pltpu.VMEM((radix - 1, left, width), jnp.bfloat16))
    each = pan // dp
    vmem = pl.BlockSpec(memory_space=pltpu.VMEM)
    return pl.pallas_call(
        functools.partial(band_kernel, dp, coef),
        out_shape=(
            jax.ShapeDtypeStruct((each, (coef // 2 + 1) * pan), jnp.float32),
            jax.ShapeDtypeStruct((each, LANES), jnp.float32),
        ),
        in_specs=[vmem] * 4,
        out_specs=(vmem, vmem),
        scratch_shapes=[pltpu.VMEM((coef // 2, rows, pan), jnp.bfloat16)]
        + buffers
        + buffers
        + [
            pltpu.SemaphoreType.DMA((coef // 2, 2)),
            pltpu.SemaphoreType.DMA((coef // 2, 2)),
            pltpu.SemaphoreType.DMA((len(WAY), 4, 3)),
            pltpu.SemaphoreType.DMA((len(WAY), 4, 3)),
        ],
        compiler_params=pltpu.CompilerParams(
            collective_id=0, has_side_effects=True, vmem_limit_bytes=48 * 1024 * 1024
        ),
    )(own, left_a, left_b, slope)


def local(location, component, epoch_bin, residual, row_scale, spatial_table, spline_table):
    dp = lax.axis_size("dp")
    me = lax.axis_index("dp")
    total_rows = location.shape[0] * dp
    scale = row_scale.astype(jnp.float32)
    row_weight = scale * (1.0 / math.sqrt(total_rows))
    own = (
        picked(spatial_table, 3 * location + component)
        * picked(spline_table, epoch_bin)
        * row_weight[:, None]
    ).astype(jnp.bfloat16)
    whitened = (scale * residual.astype(jnp.float32)).astype(jnp.bfloat16)

    left_a, left_b = (ordered(own, me, order) for order in ORDERS)
    slope = lax.dot_general(
        left_a, whitened, (((1,), (0,)), ((), ())), preferred_element_type=jnp.float32
    )
    slope = jnp.broadcast_to(slope[:, None], (slope.shape[0], LANES))
    gram_band, gradient = band(own, left_a, left_b, slope)
    return (gram_band[None], gradient[None, :, 0])


def solution(mesh):
    return jax.shard_map(
        local,
        mesh=mesh,
        in_specs=(P("dp"), P("dp"), P("dp"), P("dp"), P("dp"), P(None, "coef"), P(None, "coef")),
        out_specs=(P("coef", "dp", None), P("coef", "dp")),
        check_vma=False,
    )
```
